256 devices in a mesh: rows: 16 (over y_hi, x, core), feat: 16 (over y_lo, z).
Axes of the slice: x: 4, y: 4 (y_hi: 2, y_lo: 2; y = y_hi * 2 + y_lo), z: 8, core: 2. Of those that a mesh axis runs over, the one named last changes fastest.
Arguments:
- features: bfloat16 [3072, 16384], P('rows', 'feat'), may hold values from -0.5 to 0.5
- labels: int32 [3072], P('rows'), may hold values 0 or 1
- posterior: bfloat16 [16384], P('feat'), may hold values from -1 to 1
- prior_prec: float32 [16384], P('feat'), may hold values from 1 to 10
Outputs:
- hessian: float32 [16384, 16384], P('feat', 'rows')
- gradient: float32 [16384], P('feat')
The draws below stay inside these ranges and needn't reach their ends.
All inputs are finite; a program needn't handle non-finite values. No bound on the sum of `labels` on one device may be relied on, other than what follows from the above.
Results may differ from the reference program's by a relative error of at most 0.003.
Values may be sent and summed in bfloat16 or wider, within the bound.
No kernel may reach another device: no remote copies, remote signals or barrier semaphores. Data moves between devices by JAX's collectives and lax.ppermute only.
A program may use at most 64 MiB of HBM per device.

```python
import math
import jax
import jax.numpy as jnp
from jax import lax

F = 16384
NROWS = 3072


def plant(result, key, least, largest):
    shape = result.shape
    spot = [jax.random.randint(jax.random.fold_in(key, axis), (), 0, shape[axis]) for axis in range(len(shape))]
    result = result.at[tuple(spot)].set(least)
    longest = shape.index(max(shape))
    spot[longest] = (spot[longest] + 1) % shape[longest]
    return result.at[tuple(spot)].set(largest)


def block_scale(rng, dims, cuts, least, largest):
    def one(position, blocks):
        steps = jax.random.uniform(jax.random.fold_in(jax.random.fold_in(rng, 6), position), (blocks,), jnp.float32, least / len(cuts), largest / len(cuts))
        return jnp.repeat(jnp.exp(steps), dims[position] // blocks).reshape((-1,) + (1,) * (len(dims) - position - 1))

    loudness = one(*cuts[0])
    for cut in cuts[1:]:
        loudness = loudness * one(*cut)
    return loudness


def bell_draw(key, shape, width, bound, pieces=(), kind=jnp.bfloat16):
    entries = jax.random.normal(key, shape, jnp.float32) * width
    if len(pieces) > 0:
        entries = block_scale(key, shape, pieces, -0.22, 0.18) * entries
    return jnp.clip(entries, min=-bound, max=bound).astype(kind)


def setup_inputs(seed: int = 0) -> dict:
    splits = jax.random.split(jax.random.key(seed), 5)
    features = bell_draw(splits[0], (NROWS, F), 0.0625, 0.5, ((0, 16), (1, 16)))
    labels = plant((jax.random.randint(splits[1], (NROWS,), 0, 3) < 1).astype(jnp.int32), jax.random.fold_in(splits[1], 1), 0, 1)
    posterior = bell_draw(splits[2], (F,), (F // 512 + 1) ** -0.5, 1.0, ((0, 16),))
    prior_prec = jnp.clip(jnp.exp(math.log(10.0) - 2.3025851 * jax.random.uniform(splits[3], (F,), jnp.float32) ** block_scale(splits[3], (F,), ((0, 16),), -0.2, 0.2)), 1.0, 10.0)
    return {"features": features, "labels": labels, "posterior": posterior, "prior_prec": prior_prec}


def reference(features, labels, posterior, prior_prec):
    margins = jnp.dot(features, posterior, preferred_element_type=jnp.float32)
    chance = jax.nn.sigmoid(margins)
    weight = (chance * (1.0 - chance)).astype(jnp.bfloat16)
    residual = (labels.astype(jnp.float32) - chance).astype(jnp.bfloat16)
    gradient = jnp.dot(residual, features, preferred_element_type=jnp.float32) - prior_prec * posterior.astype(jnp.float32)
    weighted = weight[:, None] * features
    hessian = lax.dot_general(weighted, features, (((0,), (0,)), ((), ())), preferred_element_type=jnp.float32)
    diagonal = jnp.arange(F, dtype=jnp.int32)
    hessian = hessian.at[diagonal, diagonal].add(prior_prec)
    return hessian, gradient
```

```python
import jax
import jax.numpy as jnp
from jax import lax
from jax.sharding import PartitionSpec as P

SIZES = dict(yh=2, x=4, c=2, yl=2, z=8)


def place_of(index):
    r, f = divmod(index, 16)
    return dict(yh=r // 8, x=r // 2 % 4, c=r % 2, yl=f // 8, z=f % 8)


def index_of(p):
    return (p["yh"] * 8 + p["x"] * 2 + p["c"]) * 16 + p["yl"] * 8 + p["z"]


def permuted(x, move):
    pairs = []
    for i in range(256):
        p = place_of(i)
        pairs.append((i, index_of(move(p))))
    return lax.ppermute(x, ("rows", "feat"), pairs)


def shift(x, axis, by):
    def move(p):
        return {**p, axis: (p[axis] + by) % SIZES[axis]}

    return permuted(x, move)


def swap(x, axis, bit=1):
    def move(p):
        return {**p, axis: p[axis] ^ bit}

    return permuted(x, move)


def transposed(x):
    pairs = [(a * 16 + b, b * 16 + a) for a in range(16) for b in range(16)]
    return lax.ppermute(x, ("rows", "feat"), pairs)


BITS_FEAT = (("z", 1), ("z", 2), ("z", 4), ("yl", 1))
BITS_ROWS = (("c", 1), ("x", 1), ("x", 2), ("yh", 1))


def per_device(features, labels, posterior, prior_prec):
    n, width = features.shape
    a = n * 5 // 12
    row_index = lax.axis_index("rows")
    feat_index = lax.axis_index("feat")
    core, x, yh = row_index % 2, row_index // 2 % 4, row_index // 8
    z, yl = feat_index % 8, feat_index // 8

    margins = jnp.dot(features, posterior, preferred_element_type=jnp.float32)
    for axis, bit in BITS_FEAT:
        margins = margins + swap(margins, axis, bit)
    facts = jnp.stack([margins, labels.astype(jnp.float32)])
    facts = lax.dynamic_update_slice(
        jnp.zeros((16, 2, n), jnp.float32), facts[None], (row_index, 0, 0)
    )
    for axis, bit in BITS_ROWS:
        facts = facts + swap(facts, axis, bit)

    mine = transposed(features)
    first, second = mine[:a], mine[a:]
    first = jnp.stack([first, swap(first, "yl")])
    ups, downs = [first], [first]
    up_b, down_b = [second], [second]
    for k in range(1, 4):
        ups.append(shift(ups[-1], "z", 1))
        downs.append(shift(downs[-1], "z", -1))
        up_b.append(shift(up_b[-1], "z", 1))
        down_b.append(shift(down_b[-1], "z", -1))
    ups.append(shift(ups[-1], "z", 1))
    down_b.append(shift(down_b[-1], "z", -1))
    right = jnp.zeros((16, n, width), features.dtype)

    def at(yl_, z_):
        return ((z_ % 2) ^ core) * 8 + yl_ * 4 + z_ // 2

    def put(buffer, piece, yl_, z_, offset):
        return lax.dynamic_update_slice(buffer, piece[None], (at(yl_, z_), offset, 0))

    for k in range(5):
        held = [(ups[k], (z - k) % 8)]
        if 0 < k < 4:
            held.append((downs[k], (z + k) % 8))
        for pair, zz in held:
            right = put(right, pair[0], yl, zz, 0)
            right = put(right, pair[1], 1 - yl, zz, 0)
        held = [(down_b[k], (z + k) % 8)]
        if 0 < k < 4:
            held.append((up_b[k], (z - k) % 8))
        for piece, zz in held:
            right = put(right, piece, yl, zz, a)
            right = put(right, swap(piece, "yl"), 1 - yl, zz, a)

    across = swap(features, "yh")
    left_own, right_own = shift(features, "x", 1), shift(features, "x", -1)
    left_far, right_far = shift(across, "x", 1), shift(across, "x", -1)
    twice_own, twice_far = shift(left_own, "x", 1), shift(right_far, "x", -1)
    same_core = jnp.zeros((8, n, width), features.dtype)
    for piece, yh_, x_ in (
        (features, yh, x),
        (across, 1 - yh, x),
        (left_own, yh, (x + 3) % 4),
        (right_own, yh, (x + 1) % 4),
        (left_far, 1 - yh, (x + 3) % 4),
        (right_far, 1 - yh, (x + 1) % 4),
        (twice_own, yh, (x + 2) % 4),
        (twice_far, 1 - yh, (x + 2) % 4),
    ):
        same_core = lax.dynamic_update_slice(same_core, piece[None], (yh_ * 4 + x_, 0, 0))
    other_core = swap(same_core, "c")
    left = jnp.concatenate([same_core, other_core]).reshape(16 * n, width)

    by_core = facts.reshape(8, 2, 2, n).transpose(1, 2, 0, 3)
    by_core = jnp.where(core == 0, by_core, by_core[::-1])
    margins, label = by_core[:, 0].reshape(-1), by_core[:, 1].reshape(-1)
    chance = jax.nn.sigmoid(margins)
    weight = (chance * (1.0 - chance)).astype(jnp.bfloat16)
    residual = (label - chance).astype(jnp.bfloat16)

    gradient = jnp.dot(residual, left, preferred_element_type=jnp.float32)
    gradient = gradient - prior_prec * posterior.astype(jnp.float32)

    weighted = weight[:, None] * left
    product = lax.dot_general(
        weighted,
        right.reshape(16 * n, width),
        (((0,), (0,)), ((), ())),
        preferred_element_type=jnp.float32,
    )
    global_rows = feat_index * width + jnp.arange(width, dtype=jnp.int32)
    global_cols = row_index * width + jnp.arange(width, dtype=jnp.int32)
    on_diagonal = global_rows[:, None] == global_cols[None, :]
    hessian = product + jnp.where(on_diagonal, prior_prec[:, None], jnp.float32(0.0))
    return (hessian, gradient)


def solution(mesh):
    in_specs = (P("rows", "feat"), P("rows"), P("feat"), P("feat"))
    out_specs = (P("feat", "rows"), P("feat"))
    return jax.shard_map(
        per_device, mesh=mesh, in_specs=in_specs, out_specs=out_specs, check_vma=False
    )
```

```python
import jax
import jax.numpy as jnp
from jax import lax
from jax.experimental import pallas as pl
from jax.experimental.pallas import tpu as pltpu
from jax.sharding import PartitionSpec as P

SIZES = dict(yh=2, x=4, c=2, yl=2, z=8)


def place_of(index):
    r, f = divmod(index, 16)
    return dict(yh=r // 8, x=r // 2 % 4, c=r % 2, yl=f // 8, z=f % 8)


def index_of(p):
    return (p["yh"] * 8 + p["x"] * 2 + p["c"]) * 16 + p["yl"] * 8 + p["z"]


def permuted(x, move):
    pairs = [(i, index_of(move(place_of(i)))) for i in range(256)]
    return lax.ppermute(x, ("rows", "feat"), pairs)


def shift(x, axis, by):
    return permuted(x, lambda p: {**p, axis: (p[axis] + by) % SIZES[axis]})


def swap(x, axis):
    return shift(x, axis, 1)


def spread(p):
    flip = p["x"] if p["z"] % 2 == 0 else -p["x"] % 4
    z = (p["z"] + flip + 4 * p["c"]) % 8
    return dict(yh=p["yl"], x=p["z"] // 2, c=p["z"] % 2, yl=p["yh"], z=z)


def from_all(x, axis):
    copies = jnp.broadcast_to(x, (16, *x.shape))
    return lax.all_to_all(copies, axis, split_axis=0, concat_axis=0, tiled=True)


def together(*arrays):
    return lax.optimization_barrier(arrays)


def prepare_kernel(at_ref, row_ref, *refs):
    same, other = refs[0:2], refs[2:4]
    weights, residuals = refs[4:6], refs[6:8]
    out_ref, grad_ref = refs[8:]
    g = pl.program_id(0)
    n = same[0].shape[1]
    parts = []
    total = jnp.zeros(grad_ref.shape, jnp.float32)
    for i in range(2):
        block = jnp.where(at_ref[2 * g + i] < 8, same[i][0], other[i][0])
        total = total + jnp.dot(
            residuals[i][0], block, preferred_element_type=jnp.float32
        )
        parts.append(block.T.astype(jnp.float32) * weights[i][0])
    out_ref[...] = jnp.concatenate(parts, axis=1).astype(jnp.bfloat16)

    @pl.when(g == 0)
    def _():
        grad_ref[...] = jnp.zeros_like(grad_ref)

    grad_ref[...] += total


def prepare(at, row, same, other, weight, residual):
    _, n, width = same.shape

    def block(i):
        return pl.BlockSpec((1, n, width), lambda g, at, row: (at[2 * g + i] % 8, 0, 0))

    def line(i):
        return pl.BlockSpec((1, 1, n), lambda g, at, row: (row[2 * g + i], 0, 0))

    return pl.pallas_call(
        prepare_kernel,
        grid_spec=pltpu.PrefetchScalarGridSpec(
            num_scalar_prefetch=2,
            grid=(8,),
            in_specs=[block(0), block(1)] * 2 + [line(0), line(1)] * 2,
            out_specs=[
                pl.BlockSpec((width, 2 * n), lambda g, at, row: (0, g)),
                pl.BlockSpec((1, width), lambda g, at, row: (0, 0)),
            ],
        ),
        out_shape=[
            jax.ShapeDtypeStruct((width, 16 * n), jnp.bfloat16),
            jax.ShapeDtypeStruct((1, width), jnp.float32),
        ],
        compiler_params=pltpu.CompilerParams(vmem_limit_bytes=20 * 2**20),
        cost_estimate=pl.CostEstimate(
            flops=32 * n * width, bytes_accessed=96 * n * width, transcendentals=0
        ),
        name="prepare",
    )(at, row, same, same, other, other, weight, weight, residual, residual)


def gram_kernel(slots, first, n, count, has_acc, *refs):
    left_ref = refs[0]
    pieces = refs[1 : 1 + count]
    rest = refs[1 + count :]
    if has_acc:
        diag_ref, acc_ref, out_ref, lbuf, rbuf, obuf, lsem, rsem, asem, osem = rest
    else:
        out_ref, lbuf, rbuf, obuf, lsem, rsem, osem = rest
    width = obuf.shape[0]
    depth = rbuf.shape[0]
    tile = min(256, width)
    tiles = width // tile
    copies = []
    for i, (slot, offset, operand, source, rows) in enumerate(slots):
        copies.append(
            pltpu.make_async_copy(
                pieces[operand].at[pl.ds(source, rows)],
                rbuf.at[pl.ds((slot - first) * n + offset, rows)],
                rsem.at[i],
            )
        )
    lefts, accs, outs = [], [], []
    for m in range(tiles):
        ms = pl.ds(m * tile, tile)
        lefts.append(
            pltpu.make_async_copy(
                left_ref.at[ms, pl.ds(first * n, depth)], lbuf.at[ms], lsem.at[m]
            )
        )
        if has_acc:
            accs.append(pltpu.make_async_copy(acc_ref.at[ms], obuf.at[ms], asem.at[m]))
        outs.append(pltpu.make_async_copy(obuf.at[ms], out_ref.at[ms], osem.at[m]))
    lefts[0].start()
    for c in copies:
        c.start()
    for m in range(tiles):
        if m:
            lefts[m].start()
        if has_acc:
            accs[m].start()
    for c in copies:
        c.wait()
    for m in range(tiles):
        ms = pl.ds(m * tile, tile)
        lefts[m].wait()
        part = jnp.dot(lbuf[ms, :], rbuf[...], preferred_element_type=jnp.float32)
        if has_acc:
            accs[m].wait()
            obuf[ms, :] = obuf[ms, :] + part
            row = lax.broadcasted_iota(jnp.int32, (tile, tile), 0)
            col = lax.broadcasted_iota(jnp.int32, (tile, tile), 1)
            extra = jnp.where(row == col, diag_ref[:, ms], 0.0)
            obuf[ms, ms] = obuf[ms, ms] + extra
        else:
            obuf[ms, :] = part
        outs[m].start()
    for c in outs:
        c.wait()


def gram(left, slots, pieces, diag=None, acc=None):
    width = left.shape[0]
    n = left.shape[1] // 16
    first = min(slot[0] for slot in slots)
    depth = n * (1 + max(slot[0] for slot in slots) - first)
    used = sorted({slot[2] for slot in slots})
    slots = [(s, o, used.index(p), r, k) for s, o, p, r, k in slots]
    pieces = [pieces[p] for p in used]
    has_acc = acc is not None
    tiles = width // min(256, width)
    anywhere = pl.BlockSpec(memory_space=pl.ANY)
    operands = [left, *pieces]
    in_specs = [anywhere] * len(operands)
    if has_acc:
        operands += [diag, acc]
        in_specs += [pl.BlockSpec(memory_space=pltpu.VMEM), anywhere]
    sems = [pltpu.SemaphoreType.DMA((k,)) for k in [tiles, len(slots)]]
    sems += [pltpu.SemaphoreType.DMA((tiles,))] * (1 + has_acc)
    return pl.pallas_call(
        lambda *refs: gram_kernel(slots, first, n, len(pieces), has_acc, *refs),
        out_shape=jax.ShapeDtypeStruct((width, width), jnp.float32),
        in_specs=in_specs,
        out_specs=anywhere,
        scratch_shapes=[
            pltpu.VMEM((width, depth), jnp.bfloat16),
            pltpu.VMEM((depth, width), jnp.bfloat16),
            pltpu.VMEM((width, width), jnp.float32),
            *sems,
        ],
        compiler_params=pltpu.CompilerParams(vmem_limit_bytes=24 * 2**20),
        cost_estimate=pl.CostEstimate(
            flops=2 * depth * width * width,
            bytes_accessed=4 * depth * width + 4 * width * width,
            transcendentals=0,
        ),
        name="gram",
    )(*operands)


def per_device(features, labels, posterior, prior_prec):
    n, width = features.shape
    a = n * 5 // 12 // 16 * 16
    b = n - a
    row_index = lax.axis_index("rows")
    feat_index = lax.axis_index("feat")
    core, x, yh = row_index % 2, row_index // 2 % 4, row_index // 8
    z, yl = feat_index % 8, feat_index // 8

    slots, pieces, at, row = [], [], [], []

    def put(operand, *parts):
        for slot, offset, source, rows in parts:
            slots.append((slot, offset, len(pieces), source, rows))
        pieces.append(operand)

    def locate(yl_, z_):
        d = (z_ - row_index) % 8
        x_ = jnp.where(core == 0, d % 4, -d % 4)
        c_ = d // 4
        at.append((c_ ^ core) * 8 + (yl_ ^ yh) * 4 + (x_ - x) % 4)
        row.append(yl_ * 8 + x_ * 2 + c_)

    for by in (0, -1, 1, -2, 2, -3, 3, 4):
        locate(yl, (z + by) % 8)
        locate(1 - yl, (z + by) % 8)
    at = jnp.stack(at).astype(jnp.int32)
    row = jnp.stack(row).astype(jnp.int32)

    mine = permuted(features, spread)
    across = swap(features, "yh")
    margins = jnp.dot(features, posterior, preferred_element_type=jnp.float32)
    margins = from_all(margins, "feat").sum(axis=0)
    mine, across, margins = together(mine, across, margins)

    up1, down1 = shift(mine, "z", 1), shift(mine, "z", -1)
    mine_y = swap(mine, "yl")
    left1, right1 = shift(features, "x", 1), shift(features, "x", -1)
    facts = from_all(jnp.stack([margins, labels.astype(jnp.float32)]), "rows")
    up1, down1, mine_y, left1, right1, facts = together(
        up1, down1, mine_y, left1, right1, facts
    )
    put(mine, (0, 0, 0, n))
    put(mine_y, (1, 0, 0, n))

    other_a = mine_y[:a]
    up2 = shift(jnp.concatenate([up1, other_a]), "z", 1)
    down2 = shift(jnp.concatenate([down1, other_a]), "z", -1)
    swapped1 = swap(jnp.concatenate([up1[a:], down1[a:]]), "yl")
    left2, right2 = shift(across, "x", 1), shift(across, "x", -1)
    up2, down2, swapped1, left2, right2 = together(
        up2, down2, swapped1, left2, right2
    )
    put(up1, (2, 0, 0, n))
    put(down1, (4, 0, 0, n))
    put(swapped1, (3, a, 0, b), (5, a, b, b))

    up3, down3 = shift(up2, "z", 1), shift(down2, "z", -1)
    swapped2 = swap(jnp.concatenate([up2[a:n], down2[a:n]]), "yl")
    twice_own, twice_far = shift(left1, "x", 1), shift(right2, "x", -1)
    up3, down3, swapped2, twice_own, twice_far = together(
        up3, down3, swapped2, twice_own, twice_far
    )
    put(up2, (6, 0, 0, n), (3, 0, n, a))
    put(down2, (8, 0, 0, n), (5, 0, n, a))
    put(swapped2, (7, a, 0, b), (9, a, b, b))

    up4 = shift(jnp.concatenate([up3[:a], up3[n:]]), "z", 1)
    down4 = shift(down3[a:], "z", -1)
    swapped3 = swap(jnp.concatenate([up3[a:n], down3[a:n]]), "yl")
    same = [features, right1, twice_own, left1, across, right2, twice_far, left2]
    same = jnp.stack(same)
    other = swap(same, "c")
    up4, down4, swapped3, other = together(up4, down4, swapped3, other)
    put(up3, (10, 0, 0, n), (7, 0, n, a))
    put(down3, (12, 0, 0, n), (9, 0, n, a))
    put(swapped3, (11, a, 0, b), (13, a, b, b))

    up5 = shift(up4[a:], "z", 1)
    swapped4 = swap(down4[:b], "yl")
    put(up4, (14, 0, 0, a), (11, 0, a, a))
    put(down4, (14, a, 0, b), (13, 0, b, a))
    put(up5, (15, 0, 0, a))
    put(swapped4, (15, a, 0, b))

    chance = jax.nn.sigmoid(facts[:, :1])
    weight = (chance * (1.0 - chance)).astype(jnp.bfloat16).astype(jnp.float32)
    residual = (facts[:, 1:] - chance).astype(jnp.bfloat16)
    left, gradient = prepare(at, row, same, other, weight, residual)
    gradient = gradient[0] - prior_prec * posterior.astype(jnp.float32)

    diag = jnp.where(row_index == feat_index, prior_prec, 0.0)[None, :]
    early = [slot for slot in slots if slot[0] < 10]
    late = [slot for slot in slots if slot[0] >= 10]
    acc = gram(left, early, pieces)
    hessian = gram(left, late, pieces, diag, acc)
    return (hessian, gradient)


def solution(mesh):
    in_specs = (P("rows", "feat"), P("rows"), P("feat"), P("feat"))
    out_specs = (P("feat", "rows"), P("feat"))
    return jax.shard_map(
        per_device, mesh=mesh, in_specs=in_specs, out_specs=out_specs, check_vma=False
    )
```

```python
import jax
import jax.numpy as jnp
from jax import lax
from jax.experimental import pallas as pl
from jax.experimental.pallas import tpu as pltpu
from jax.sharding import PartitionSpec as P

SIZES = dict(yh=2, x=4, c=2, yl=2, z=8)


def place_of(index):
    r, f = divmod(index, 16)
    return dict(yh=r // 8, x=r // 2 % 4, c=r % 2, yl=f // 8, z=f % 8)


def index_of(p):
    return (p["yh"] * 8 + p["x"] * 2 + p["c"]) * 16 + p["yl"] * 8 + p["z"]


def permuted(x, move):
    pairs = [(i, index_of(move(place_of(i)))) for i in range(256)]
    return lax.ppermute(x, ("rows", "feat"), pairs)


def shift(x, axis, by):
    return permuted(x, lambda p: {**p, axis: (p[axis] + by) % SIZES[axis]})


def swap(x, axis):
    return shift(x, axis, 1)


def spread(p):
    flip = p["x"] if p["z"] % 2 == 0 else -p["x"] % 4
    z = (p["z"] + flip + 4 * p["c"]) % 8
    return dict(yh=p["yl"], x=p["z"] // 2, c=p["z"] % 2, yl=p["yh"], z=z)


def from_all(x, axis):
    copies = jnp.broadcast_to(x, (16, *x.shape))
    return lax.all_to_all(copies, axis, split_axis=0, concat_axis=0, tiled=True)


def together(*arrays):
    return lax.optimization_barrier(arrays)


def prepare_kernel(slot_ref, row_ref, *refs):
    same, other = refs[:2]
    weight_ref, residual_ref, prior_ref, point_ref = refs[2:6]
    out_ref, grad_ref, lbuf, obuf, lsem, osem = refs[6:]
    _, n, width = same.shape
    copies = []
    for i in range(16):
        start = pl.multiple_of(slot_ref[i] * n, 16)
        copies.append(
            pltpu.make_async_copy(
                (same if i < 8 else other).at[i % 8],
                lbuf.at[pl.ds(start, n)],
                lsem.at[i],
            )
        )
    for c in copies:
        c.start()
    for c in copies:
        c.wait()
    total = jnp.zeros(grad_ref.shape, jnp.float32)
    outs = []
    for g in range(8):
        block = lbuf[2 * g * n : 2 * (g + 1) * n, :]
        lines = [residual_ref[row_ref[2 * g + i]] for i in range(2)]
        total = total + jnp.dot(
            jnp.concatenate(lines, axis=1), block, preferred_element_type=jnp.float32
        )
        scales = [weight_ref[row_ref[2 * g + i]] for i in range(2)]
        turned = block.T.astype(jnp.float32) * jnp.concatenate(scales, axis=1)
        columns = pl.ds(2 * g * n, 2 * n)
        obuf[:, columns] = turned.astype(jnp.bfloat16)
        outs.append(
            pltpu.make_async_copy(
                obuf.at[:, columns], out_ref.at[:, columns], osem.at[g]
            )
        )
        outs[-1].start()
    grad_ref[...] = total - prior_ref[...] * point_ref[...].astype(jnp.float32)
    for c in outs:
        c.wait()


def prepare(slot, row, same, other, weight, residual, prior, point):
    _, n, width = same.shape
    smem = pl.BlockSpec(memory_space=pltpu.SMEM)
    vmem = pl.BlockSpec(memory_space=pltpu.VMEM)
    anywhere = pl.BlockSpec(memory_space=pl.ANY)
    return pl.pallas_call(
        prepare_kernel,
        in_specs=[smem, smem] + [anywhere] * 2 + [vmem] * 4,
        out_specs=[pl.BlockSpec(memory_space=pltpu.HBM), vmem],
        out_shape=[
            jax.ShapeDtypeStruct((width, 16 * n), jnp.bfloat16),
            jax.ShapeDtypeStruct((1, width), jnp.float32),
        ],
        scratch_shapes=[
            pltpu.VMEM((16 * n, width), jnp.bfloat16),
            pltpu.VMEM((width, 16 * n), jnp.bfloat16),
            pltpu.SemaphoreType.DMA((16,)),
            pltpu.SemaphoreType.DMA((8,)),
        ],
        compiler_params=pltpu.CompilerParams(vmem_limit_bytes=60 * 2**20),
        cost_estimate=pl.CostEstimate(flops=1, bytes_accessed=1, transcendentals=0),
        name="prepare",
    )(slot, row, same, other, weight, residual, prior, point)


def gram_kernel(slots, first, n, count, has_acc, has_diag, *refs):
    left_ref = refs[0]
    pieces = refs[1 : 1 + count]
    rest = refs[1 + count :]
    if has_acc:
        acc_ref, rest = rest[0], rest[1:]
    if has_diag:
        diag_ref, rest = rest[0], rest[1:]
    out_ref, lbuf, rbuf, obuf, lsem, rsem, asem, osem = rest
    width = obuf.shape[0]
    depth = rbuf.shape[0]
    tile = min(256, width)
    tiles = width // tile
    copies = []
    for i, (slot, offset, operand, source, rows) in enumerate(slots):
        copies.append(
            pltpu.make_async_copy(
                pieces[operand].at[pl.ds(source, rows)],
                rbuf.at[pl.ds((slot - first) * n + offset, rows)],
                rsem.at[i],
            )
        )
    lefts, accs, outs = [], [], []
    for m in range(tiles):
        ms = pl.ds(m * tile, tile)
        lefts.append(
            pltpu.make_async_copy(
                left_ref.at[ms, pl.ds(first * n, depth)], lbuf.at[ms], lsem.at[m]
            )
        )
        if has_acc:
            accs.append(pltpu.make_async_copy(acc_ref.at[ms], obuf.at[ms], asem.at[m]))
        outs.append(pltpu.make_async_copy(obuf.at[ms], out_ref.at[ms], osem.at[m]))
    lefts[0].start()
    for c in copies:
        c.start()
    for m in range(tiles):
        if m:
            lefts[m].start()
        if has_acc:
            accs[m].start()
    for c in copies:
        c.wait()
    for m in range(tiles):
        ms = pl.ds(m * tile, tile)
        lefts[m].wait()
        part = jnp.dot(lbuf[ms, :], rbuf[...], preferred_element_type=jnp.float32)
        if has_acc:
            accs[m].wait()
            obuf[ms, :] = obuf[ms, :] + part
        else:
            obuf[ms, :] = part
        if has_diag:
            row = lax.broadcasted_iota(jnp.int32, (tile, tile), 0)
            col = lax.broadcasted_iota(jnp.int32, (tile, tile), 1)
            extra = jnp.where(row == col, diag_ref[:, ms], 0.0)
            obuf[ms, ms] = obuf[ms, ms] + extra
        outs[m].start()
    for c in outs:
        c.wait()


def gram(left, slots, pieces, acc=None, diag=None):
    width = left.shape[0]
    n = left.shape[1] // 16
    first = min(slot[0] for slot in slots)
    depth = n * (1 + max(slot[0] for slot in slots) - first)
    used = sorted({slot[2] for slot in slots})
    slots = [(s, o, used.index(p), r, k) for s, o, p, r, k in slots]
    pieces = [pieces[p] for p in used]
    has_acc, has_diag = acc is not None, diag is not None
    tiles = width // min(256, width)
    anywhere = pl.BlockSpec(memory_space=pl.ANY)
    operands = [left, *pieces]
    far = pl.BlockSpec(memory_space=pltpu.HBM)
    in_specs = [far] + [anywhere] * len(pieces)
    if has_acc:
        operands.append(acc)
        in_specs.append(far)
    if has_diag:
        operands.append(diag)
        in_specs.append(pl.BlockSpec(memory_space=pltpu.VMEM))
    sems = [pltpu.SemaphoreType.DMA((k,)) for k in [tiles, len(slots)]]
    sems += [pltpu.SemaphoreType.DMA((tiles,))] * 2
    return pl.pallas_call(
        lambda *refs: gram_kernel(slots, first, n, len(pieces), has_acc, has_diag, *refs),
        out_shape=jax.ShapeDtypeStruct((width, width), jnp.float32),
        in_specs=in_specs,
        out_specs=far,
        scratch_shapes=[
            pltpu.VMEM((width, depth), jnp.bfloat16),
            pltpu.VMEM((depth, width), jnp.bfloat16),
            pltpu.VMEM((width, width), jnp.float32),
            *sems,
        ],
        compiler_params=pltpu.CompilerParams(vmem_limit_bytes=60 * 2**20),
        cost_estimate=pl.CostEstimate(flops=1, bytes_accessed=1, transcendentals=0),
        name="gram",
    )(*operands)


def per_device(features, labels, posterior, prior_prec):
    n, width = features.shape
    a = n * 5 // 12 // 16 * 16
    b = n - a
    row_index = lax.axis_index("rows")
    feat_index = lax.axis_index("feat")
    core, x, yh = row_index % 2, row_index // 2 % 4, row_index // 8
    z, yl = feat_index % 8, feat_index // 8

    slots, pieces, row = [], [], []

    def put(operand, *parts):
        for slot, offset, source, rows in parts:
            slots.append((slot, offset, len(pieces), source, rows))
        pieces.append(operand)

    for by in (0, -1, 1, -2, 2, -3, 3, 4):
        for yl_ in (yl, 1 - yl):
            d = ((z + by) - row_index) % 8
            x_ = jnp.where(core == 0, d % 4, -d % 4)
            row.append(yl_ * 8 + x_ * 2 + d // 4)
    row = jnp.stack(row).astype(jnp.int32)

    def slot_of(other, dy, dx):
        c_, x_ = core ^ other, (x + dx) % 4
        d = c_ * 4 + jnp.where(core == 0, x_, -x_ % 4)
        by = (d + row_index - z + 3) % 8 - 3
        rank = jnp.where(by < 0, -2 * by - 1, 2 * by)
        rank = jnp.where(by == 4, 7, rank)
        return 2 * rank + (yh ^ dy ^ yl)

    order = [(0, 0), (0, 1), (0, 3), (1, 0), (1, 1), (1, 3), (0, 2), (1, 2)]
    slot = [slot_of(other, dy, dx) for other in range(2) for dy, dx in order]
    slot = jnp.stack(slot).astype(jnp.int32)

    mine = permuted(features, spread)
    partial = jnp.dot(features, posterior, preferred_element_type=jnp.float32)
    across = swap(features, "yh")
    left1, right1 = shift(features, "x", 1), shift(features, "x", -1)
    margins = from_all(partial, "feat").sum(axis=0)
    across, left1, right1, margins, mine = together(
        across, left1, right1, margins, mine
    )

    up1, down1 = shift(mine, "z", 1), shift(mine, "z", -1)
    mine_y = swap(mine, "yl")
    left2, right2 = shift(across, "x", 1), shift(across, "x", -1)
    facts = jnp.stack([margins, labels.astype(jnp.float32)])
    facts = from_all(facts, "rows")
    up1, down1, mine_y, left2, right2, facts = together(
        up1, down1, mine_y, left2, right2, facts
    )
    put(mine, (0, 0, 0, n))
    put(mine_y, (1, 0, 0, n))

    other_a = mine_y[:a]
    up2 = shift(jnp.concatenate([up1[:a], other_a, up1[a:]]), "z", 1)
    down2 = shift(jnp.concatenate([down1, other_a]), "z", -1)
    swapped1 = swap(jnp.concatenate([up1[a:], down1[a:]]), "yl")
    twice_own, twice_far = shift(left1, "x", 1), shift(right2, "x", -1)
    up2, down2, swapped1, twice_own, twice_far = together(
        up2, down2, swapped1, twice_own, twice_far
    )
    put(up1, (2, 0, 0, n))
    put(down1, (4, 0, 0, n))
    put(swapped1, (3, a, 0, b), (5, a, b, b))

    up3, down3 = shift(up2, "z", 1), shift(down2, "z", -1)
    swap_u2, swap_d2 = swap(up2[2 * a :], "yl"), swap(down2[a:n], "yl")
    same = [features, right1, left1, across, right2, left2, twice_own, twice_far]
    same = jnp.stack(same)
    other = swap(same, "c")
    chance = jax.nn.sigmoid(facts[:, :1])
    weight = (chance * (1.0 - chance)).astype(jnp.bfloat16).astype(jnp.float32)
    residual = (facts[:, 1:] - chance).astype(jnp.bfloat16)
    left, gradient = prepare(
        slot, row, same, other, weight, residual, prior_prec[None], posterior[None]
    )
    up3, down3, swap_u2, swap_d2, left = together(up3, down3, swap_u2, swap_d2, left)
    put(up2, (6, 0, 0, a), (3, 0, a, a), (6, a, 2 * a, b))
    put(down2, (8, 0, 0, n), (5, 0, n, a))
    put(swap_u2, (7, a, 0, b))
    put(swap_d2, (9, a, 0, b))

    up4 = shift(up3[: 2 * a], "z", 1)
    down4 = shift(down3[a:], "z", -1)
    swap_u3, swap_d3 = swap(up3[2 * a :], "yl"), swap(down3[a:n], "yl")
    put(up3, (10, 0, 0, a), (7, 0, a, a), (10, a, 2 * a, b))
    put(down3, (12, 0, 0, n), (9, 0, n, a))
    put(swap_u3, (11, a, 0, b))
    put(swap_d3, (13, a, 0, b))
    acc = gram(left, [slot for slot in slots if slot[0] < 10], pieces)
    up4, down4, swap_u3, swap_d3, acc = together(up4, down4, swap_u3, swap_d3, acc)

    up5 = shift(up4[a:], "z", 1)
    swapped4 = swap(down4[:b], "yl")
    pieces[-2:] = [swap_u3, swap_d3]
    put(up4, (14, 0, 0, a), (11, 0, a, a))
    put(down4, (14, a, 0, b), (13, 0, b, a))
    acc = gram(left, [slot for slot in slots if 10 <= slot[0] < 14], pieces, acc)
    put(up5, (15, 0, 0, a))
    put(swapped4, (15, a, 0, b))

    diag = jnp.where(row_index == feat_index, prior_prec, 0.0)[None, :]
    last = [slot for slot in slots if slot[0] >= 14]
    hessian = gram(left, last, pieces, acc, diag)
    return (hessian, gradient[0])


def solution(mesh):
    in_specs = (P("rows", "feat"), P("rows"), P("feat"), P("feat"))
    out_specs = (P("feat", "rows"), P("feat"))
    return jax.shard_map(
        per_device, mesh=mesh, in_specs=in_specs, out_specs=out_specs, check_vma=False
    )
```

```python
import jax
import jax.numpy as jnp
from jax import lax
from jax.experimental import pallas as pl
from jax.experimental.pallas import tpu as pltpu
from jax.sharding import PartitionSpec as P

SIZES = dict(yh=2, x=4, c=2, yl=2, z=8)


def place_of(index):
    r, f = divmod(index, 16)
    return dict(yh=r // 8, x=r // 2 % 4, c=r % 2, yl=f // 8, z=f % 8)


def index_of(p):
    return (p["yh"] * 8 + p["x"] * 2 + p["c"]) * 16 + p["yl"] * 8 + p["z"]


def permuted(x, move):
    pairs = [(i, index_of(move(place_of(i)))) for i in range(256)]
    return lax.ppermute(x, ("rows", "feat"), pairs)


def shift(x, axis, by):
    return permuted(x, lambda p: {**p, axis: (p[axis] + by) % SIZES[axis]})


def swap(x, axis):
    return shift(x, axis, 1)


def spread(p):
    flip = p["x"] if p["z"] % 2 == 0 else -p["x"] % 4
    z = (p["z"] + flip + 4 * p["c"]) % 8
    return dict(yh=p["yl"], x=p["z"] // 2, c=p["z"] % 2, yl=p["yh"], z=z)


def from_all(x, axis):
    copies = jnp.broadcast_to(x, (16, *x.shape))
    return lax.all_to_all(copies, axis, split_axis=0, concat_axis=0, tiled=True)


def together(*arrays):
    return lax.optimization_barrier(arrays)


def prepare_kernel(slot_ref, row_ref, *refs):
    same, other = refs[:2]
    weight_ref, residual_ref, prior_ref, point_ref = refs[2:6]
    out_ref, grad_ref, lbuf, obuf, lsem, osem = refs[6:]
    _, n, width = same.shape
    copies = []
    for i in range(16):
        start = pl.multiple_of(slot_ref[i] * n, 16)
        copies.append(
            pltpu.make_async_copy(
                (same if i < 8 else other).at[i % 8],
                lbuf.at[pl.ds(start, n)],
                lsem.at[i],
            )
        )
    for c in copies:
        c.start()
    for c in copies:
        c.wait()
    total = jnp.zeros(grad_ref.shape, jnp.float32)
    outs = []
    for g in range(8):
        block = lbuf[2 * g * n : 2 * (g + 1) * n, :]
        lines = [residual_ref[row_ref[2 * g + i]] for i in range(2)]
        total = total + jnp.dot(
            jnp.concatenate(lines, axis=1), block, preferred_element_type=jnp.float32
        )
        scales = [weight_ref[row_ref[2 * g + i]] for i in range(2)]
        turned = block.T.astype(jnp.float32) * jnp.concatenate(scales, axis=1)
        columns = pl.ds(2 * g * n, 2 * n)
        obuf[:, columns] = turned.astype(jnp.bfloat16)
        outs.append(
            pltpu.make_async_copy(
                obuf.at[:, columns], out_ref.at[:, columns], osem.at[g]
            )
        )
        outs[-1].start()
    grad_ref[...] = total - prior_ref[...] * point_ref[...].astype(jnp.float32)
    for c in outs:
        c.wait()


def prepare(slot, row, same, other, weight, residual, prior, point):
    _, n, width = same.shape
    smem = pl.BlockSpec(memory_space=pltpu.SMEM)
    vmem = pl.BlockSpec(memory_space=pltpu.VMEM)
    anywhere = pl.BlockSpec(memory_space=pl.ANY)
    return pl.pallas_call(
        prepare_kernel,
        in_specs=[smem, smem] + [anywhere] * 2 + [vmem] * 4,
        out_specs=[pl.BlockSpec(memory_space=pltpu.HBM), vmem],
        out_shape=[
            jax.ShapeDtypeStruct((width, 16 * n), jnp.bfloat16),
            jax.ShapeDtypeStruct((1, width), jnp.float32),
        ],
        scratch_shapes=[
            pltpu.VMEM((16 * n, width), jnp.bfloat16),
            pltpu.VMEM((width, 16 * n), jnp.bfloat16),
            pltpu.SemaphoreType.DMA((16,)),
            pltpu.SemaphoreType.DMA((8,)),
        ],
        compiler_params=pltpu.CompilerParams(vmem_limit_bytes=60 * 2**20),
        cost_estimate=pl.CostEstimate(flops=1, bytes_accessed=1, transcendentals=0),
        name="prepare",
    )(slot, row, same, other, weight, residual, prior, point)


def gram_kernel(slots, first, n, count, cuts, has_acc, has_diag, *refs):
    left_ref = refs[0]
    pieces = refs[1 : 1 + count]
    rest = refs[1 + count :]
    if has_acc:
        acc_ref, rest = rest[0], rest[1:]
    if has_diag:
        diag_ref, rest = rest[0], rest[1:]
    out_ref, lbuf, rbuf, tbuf, abuf, obuf, lsem, rsem, asem, osem = rest
    width = obuf.shape[0]
    tile = min(256, width)
    tiles = width // tile
    spans = list(zip(cuts[:-1], cuts[1:]))
    copies = [[] for _ in spans]
    for i, (slot, offset, operand, source, rows) in enumerate(slots):
        at = (slot - first) * n + offset
        span = [k for k, (lo, hi) in enumerate(spans) if lo <= at < hi][0]
        copies[span].append(
            pltpu.make_async_copy(
                pieces[operand].at[pl.ds(source, rows)],
                rbuf.at[pl.ds(at, rows)],
                rsem.at[i],
            )
        )
    lefts, accs, outs = [], [], []
    for m in range(tiles):
        ms = pl.ds(m * tile, tile)
        for k, (lo, hi) in enumerate(spans):
            lefts.append(
                pltpu.make_async_copy(
                    left_ref.at[ms, pl.ds(first * n + lo, hi - lo)],
                    lbuf.at[ms, pl.ds(lo, hi - lo)],
                    lsem.at[m * len(spans) + k],
                )
            )
        if has_acc:
            accs.append(pltpu.make_async_copy(acc_ref.at[ms], abuf.at[ms], asem.at[m]))
        outs.append(pltpu.make_async_copy(obuf.at[ms], out_ref.at[ms], osem.at[m]))
    for k in range(len(spans)):
        lefts[k].start()
        for c in copies[k]:
            c.start()
        for m in range(1, tiles):
            lefts[m * len(spans) + k].start()
    for c in accs:
        c.start()
    for k, (lo, hi) in enumerate(spans):
        for c in copies[k]:
            c.wait()
        for m in range(tiles):
            ms = pl.ds(m * tile, tile)
            lefts[m * len(spans) + k].wait()
            part = jnp.dot(
                lbuf[ms, lo:hi], rbuf[lo:hi, :], preferred_element_type=jnp.float32
            )
            if k:
                part = part + tbuf[ms, :]
            if k < len(spans) - 1:
                tbuf[ms, :] = part
                continue
            if has_acc:
                accs[m].wait()
                part = part + abuf[ms, :].astype(jnp.float32)
            obuf[ms, :] = part.astype(obuf.dtype)
            if has_diag:
                row = lax.broadcasted_iota(jnp.int32, (tile, tile), 0)
                col = lax.broadcasted_iota(jnp.int32, (tile, tile), 1)
                extra = jnp.where(row == col, diag_ref[:, ms], 0.0)
                obuf[ms, ms] = obuf[ms, ms] + extra
            outs[m].start()
    for c in outs:
        c.wait()


def gram(left, slots, pieces, acc=None, diag=None):
    width = left.shape[0]
    n = left.shape[1] // 16
    first = min(slot[0] for slot in slots)
    depth = n * (1 + max(slot[0] for slot in slots) - first)
    cuts = [0, 6 * n, depth] if depth > 6 * n else [0, depth]
    used = sorted({slot[2] for slot in slots})
    slots = [(s, o, used.index(p), r, k) for s, o, p, r, k in slots]
    pieces = [pieces[p] for p in used]
    has_acc, has_diag = acc is not None, diag is not None
    kind = jnp.float32 if has_diag else jnp.bfloat16
    tiles = width // min(256, width)
    anywhere = pl.BlockSpec(memory_space=pl.ANY)
    operands = [left, *pieces]
    in_specs = [anywhere] * len(operands)
    if has_acc:
        operands.append(acc)
        in_specs.append(anywhere)
    if has_diag:
        operands.append(diag)
        in_specs.append(pl.BlockSpec(memory_space=pltpu.VMEM))
    sems = [tiles * (len(cuts) - 1), len(slots), tiles, tiles]
    return pl.pallas_call(
        lambda *refs: gram_kernel(
            slots, first, n, len(pieces), cuts, has_acc, has_diag, *refs
        ),
        out_shape=jax.ShapeDtypeStruct((width, width), kind),
        in_specs=in_specs,
        out_specs=anywhere,
        scratch_shapes=[
            pltpu.VMEM((width, depth), jnp.bfloat16),
            pltpu.VMEM((depth, width), jnp.bfloat16),
            pltpu.VMEM((width if len(cuts) > 2 else 8, width), jnp.float32),
            pltpu.VMEM((width if has_acc else 16, width), jnp.bfloat16),
            pltpu.VMEM((width, width), kind),
            *[pltpu.SemaphoreType.DMA((k,)) for k in sems],
        ],
        compiler_params=pltpu.CompilerParams(vmem_limit_bytes=60 * 2**20),
        cost_estimate=pl.CostEstimate(flops=1, bytes_accessed=1, transcendentals=0),
        name="gram",
    )(*operands)


def per_device(features, labels, posterior, prior_prec):
    n, width = features.shape
    a = n * 5 // 12 // 16 * 16
    b = n - a
    row_index = lax.axis_index("rows")
    feat_index = lax.axis_index("feat")
    core, x, yh = row_index % 2, row_index // 2 % 4, row_index // 8
    z, yl = feat_index % 8, feat_index // 8

    slots, pieces, row = [], [], []

    def put(operand, *parts):
        for slot, offset, source, rows in parts:
            slots.append((slot, offset, len(pieces), source, rows))
        pieces.append(operand)

    for by in (0, -1, 1, -2, 2, -3, 3, 4):
        for yl_ in (yl, 1 - yl):
            d = ((z + by) - row_index) % 8
            x_ = jnp.where(core == 0, d % 4, -d % 4)
            row.append(yl_ * 8 + x_ * 2 + d // 4)
    row = jnp.stack(row).astype(jnp.int32)

    def slot_of(other, dy, dx):
        c_, x_ = core ^ other, (x + dx) % 4
        d = c_ * 4 + jnp.where(core == 0, x_, -x_ % 4)
        by = (d + row_index - z + 3) % 8 - 3
        rank = jnp.where(by < 0, -2 * by - 1, 2 * by)
        rank = jnp.where(by == 4, 7, rank)
        return 2 * rank + (yh ^ dy ^ yl)

    order = [(0, 0), (0, 1), (0, 3), (1, 0), (1, 1), (1, 3), (0, 2), (1, 2)]
    slot = [slot_of(other, dy, dx) for other in range(2) for dy, dx in order]
    slot = jnp.stack(slot).astype(jnp.int32)

    mine = permuted(features, spread)
    partial = jnp.dot(features, posterior, preferred_element_type=jnp.float32)
    across = swap(features, "yh")
    left1, right1 = shift(features, "x", 1), shift(features, "x", -1)
    margins = from_all(partial, "feat").sum(axis=0)
    across, left1, right1, margins, mine = together(
        across, left1, right1, margins, mine
    )

    up1, down1 = shift(mine, "z", 1), shift(mine, "z", -1)
    mine_y = swap(mine, "yl")
    left2, right2 = shift(across, "x", 1), shift(across, "x", -1)
    facts = jnp.stack([margins, labels.astype(jnp.float32)])
    facts = from_all(facts, "rows")
    up1, down1, mine_y, left2, right2, facts = together(
        up1, down1, mine_y, left2, right2, facts
    )
    chance = jax.nn.sigmoid(facts[:, :1])
    weight = (chance * (1.0 - chance)).astype(jnp.bfloat16).astype(jnp.float32)
    residual = (facts[:, 1:] - chance).astype(jnp.bfloat16)
    diag = jnp.where(row_index == feat_index, prior_prec, 0.0)[None, :]
    put(mine, (0, 0, 0, n))
    put(mine_y, (1, 0, 0, n))

    other_a = mine_y[:a]
    up2 = shift(jnp.concatenate([up1[:a], other_a, up1[a:]]), "z", 1)
    down2 = shift(jnp.concatenate([down1, other_a]), "z", -1)
    swapped1 = swap(jnp.concatenate([up1[a:], down1[a:]]), "yl")
    twice_own, twice_far = shift(left1, "x", 1), shift(right2, "x", -1)
    up2, down2, swapped1, twice_own, twice_far, *small = together(
        up2, down2, swapped1, twice_own, twice_far, weight, residual, diag, slot, row
    )
    weight, residual, diag, slot, row = small
    put(up1, (2, 0, 0, n))
    put(down1, (4, 0, 0, n))
    put(swapped1, (3, a, 0, b), (5, a, b, b))

    up3, down3 = shift(up2, "z", 1), shift(down2, "z", -1)
    swap_u2, swap_d2 = swap(up2[2 * a :], "yl"), swap(down2[a:n], "yl")
    same = [features, right1, left1, across, right2, left2, twice_own, twice_far]
    same = jnp.stack(same)
    other = swap(same, "c")
    left, gradient = prepare(
        slot, row, same, other, weight, residual, prior_prec[None], posterior[None]
    )
    up3, down3, swap_u2, swap_d2, left = together(up3, down3, swap_u2, swap_d2, left)
    put(up2, (6, 0, 0, a), (3, 0, a, a), (6, a, 2 * a, b))
    put(down2, (8, 0, 0, n), (5, 0, n, a))
    put(swap_u2, (7, a, 0, b))
    put(swap_d2, (9, a, 0, b))

    up4 = shift(up3[: 2 * a], "z", 1)
    down4 = shift(down3[a:], "z", -1)
    swap_u3, swap_d3 = swap(up3[2 * a :], "yl"), swap(down3[a:n], "yl")
    put(up3, (10, 0, 0, a), (7, 0, a, a), (10, a, 2 * a, b))
    put(down3, (12, 0, 0, n), (9, 0, n, a))
    put(swap_u3, (11, a, 0, b))
    put(swap_d3, (13, a, 0, b))
    acc = gram(left, [slot for slot in slots if slot[0] < 10], pieces)
    up4, down4, swap_u3, swap_d3, acc = together(up4, down4, swap_u3, swap_d3, acc)

    up5 = shift(up4[a:], "z", 1)
    swapped4 = swap(down4[:b], "yl")
    pieces[-2:] = [swap_u3, swap_d3]
    put(up4, (14, 0, 0, a), (11, 0, a, a))
    put(down4, (14, a, 0, b), (13, 0, b, a))
    acc = gram(left, [slot for slot in slots if 10 <= slot[0] < 14], pieces, acc)
    put(up5, (15, 0, 0, a))
    put(swapped4, (15, a, 0, b))

    last = [slot for slot in slots if slot[0] >= 14]
    hessian = gram(left, last, pieces, acc, diag)
    return (hessian, gradient[0])


def solution(mesh):
    in_specs = (P("rows", "feat"), P("rows"), P("feat"), P("feat"))
    out_specs = (P("feat", "rows"), P("feat"))
    return jax.shard_map(
        per_device, mesh=mesh, in_specs=in_specs, out_specs=out_specs, check_vma=False
    )
```

```python
import jax
import jax.numpy as jnp
from jax import lax
from jax.experimental import pallas as pl
from jax.experimental.pallas import tpu as pltpu
from jax.sharding import PartitionSpec as P

SIZES = dict(yh=2, x=4, c=2, yl=2, z=8)


def place_of(index):
    r, f = divmod(index, 16)
    return dict(yh=r // 8, x=r // 2 % 4, c=r % 2, yl=f // 8, z=f % 8)


def index_of(p):
    return (p["yh"] * 8 + p["x"] * 2 + p["c"]) * 16 + p["yl"] * 8 + p["z"]


def permuted(x, move):
    pairs = [(i, index_of(move(place_of(i)))) for i in range(256)]
    return lax.ppermute(x, ("rows", "feat"), pairs)


def shift(x, axis, by):
    return permuted(x, lambda p: {**p, axis: (p[axis] + by) % SIZES[axis]})


def swap(x, axis):
    return shift(x, axis, 1)


def spread(p):
    flip = p["x"] if p["z"] % 2 == 0 else -p["x"] % 4
    z = (p["z"] + flip + 4 * p["c"]) % 8
    return dict(yh=p["yl"], x=p["z"] // 2, c=p["z"] % 2, yl=p["yh"], z=z)


def from_all(x, axis):
    copies = jnp.broadcast_to(x, (16, *x.shape))
    return lax.all_to_all(copies, axis, split_axis=0, concat_axis=0, tiled=True)


def together(*arrays):
    return lax.optimization_barrier(arrays)


def prepare_kernel(slot_ref, row_ref, *refs):
    same, other = refs[:2]
    weight_ref, residual_ref, prior_ref, point_ref = refs[2:6]
    out_ref, grad_ref, lbuf, obuf, lsem, osem = refs[6:]
    _, n, width = same.shape
    copies = []
    for i in range(16):
        start = pl.multiple_of(slot_ref[i] * n, 16)
        copies.append(
            pltpu.make_async_copy(
                (same if i < 8 else other).at[i % 8],
                lbuf.at[pl.ds(start, n)],
                lsem.at[i],
            )
        )
    for c in copies:
        c.start()
    for c in copies:
        c.wait()
    total = jnp.zeros(grad_ref.shape, jnp.float32)
    outs = []
    for g in range(8):
        block = lbuf[2 * g * n : 2 * (g + 1) * n, :]
        lines = [residual_ref[row_ref[2 * g + i]] for i in range(2)]
        total = total + jnp.dot(
            jnp.concatenate(lines, axis=1), block, preferred_element_type=jnp.float32
        )
        scales = [weight_ref[row_ref[2 * g + i]] for i in range(2)]
        turned = block.T.astype(jnp.float32) * jnp.concatenate(scales, axis=1)
        columns = pl.ds(2 * g * n, 2 * n)
        obuf[:, columns] = turned.astype(jnp.bfloat16)
        outs.append(
            pltpu.make_async_copy(
                obuf.at[:, columns], out_ref.at[:, columns], osem.at[g]
            )
        )
        outs[-1].start()
    grad_ref[...] = total - prior_ref[...] * point_ref[...].astype(jnp.float32)
    for c in outs:
        c.wait()


def prepare(slot, row, same, other, weight, residual, prior, point):
    _, n, width = same.shape
    smem = pl.BlockSpec(memory_space=pltpu.SMEM)
    vmem = pl.BlockSpec(memory_space=pltpu.VMEM)
    anywhere = pl.BlockSpec(memory_space=pl.ANY)
    return pl.pallas_call(
        prepare_kernel,
        in_specs=[smem, smem] + [anywhere] * 2 + [vmem] * 4,
        out_specs=[pl.BlockSpec(memory_space=pltpu.HBM), vmem],
        out_shape=[
            jax.ShapeDtypeStruct((width, 16 * n), jnp.bfloat16),
            jax.ShapeDtypeStruct((1, width), jnp.float32),
        ],
        scratch_shapes=[
            pltpu.VMEM((16 * n, width), jnp.bfloat16),
            pltpu.VMEM((width, 16 * n), jnp.bfloat16),
            pltpu.SemaphoreType.DMA((16,)),
            pltpu.SemaphoreType.DMA((8,)),
        ],
        compiler_params=pltpu.CompilerParams(vmem_limit_bytes=60 * 2**20),
        cost_estimate=pl.CostEstimate(flops=1, bytes_accessed=1, transcendentals=0),
        name="prepare",
    )(slot, row, same, other, weight, residual, prior, point)


def gram_kernel(slots, first, n, count, cuts, has_acc, has_diag, *refs):
    left_ref = refs[0]
    pieces = refs[1 : 1 + count]
    rest = refs[1 + count :]
    if has_acc:
        acc_ref, rest = rest[0], rest[1:]
    if has_diag:
        diag_ref, rest = rest[0], rest[1:]
    out_ref, lbuf, rbuf, tbuf, abuf, obuf, lsem, rsem, asem, osem = rest
    width = obuf.shape[0]
    tile = min(256, width)
    tiles = width // tile
    spans = list(zip(cuts[:-1], cuts[1:]))
    copies = [[] for _ in spans]
    for i, (slot, offset, operand, source, rows) in enumerate(slots):
        at = (slot - first) * n + offset
        span = [k for k, (lo, hi) in enumerate(spans) if lo <= at < hi][0]
        copies[span].append(
            pltpu.make_async_copy(
                pieces[operand].at[pl.ds(source, rows)],
                rbuf.at[pl.ds(at, rows)],
                rsem.at[i],
            )
        )
    lefts, accs, outs = [], [], []
    for m in range(tiles):
        ms = pl.ds(m * tile, tile)
        for k, (lo, hi) in enumerate(spans):
            lefts.append(
                pltpu.make_async_copy(
                    left_ref.at[ms, pl.ds(first * n + lo, hi - lo)],
                    lbuf.at[ms, pl.ds(lo, hi - lo)],
                    lsem.at[m * len(spans) + k],
                )
            )
        if has_acc:
            accs.append(pltpu.make_async_copy(acc_ref.at[ms], abuf.at[ms], asem.at[m]))
        outs.append(pltpu.make_async_copy(obuf.at[ms], out_ref.at[ms], osem.at[m]))
    for k in range(len(spans)):
        lefts[k].start()
        for c in copies[k]:
            c.start()
        for m in range(1, tiles):
            lefts[m * len(spans) + k].start()
    for c in accs:
        c.start()
    for k, (lo, hi) in enumerate(spans):
        for c in copies[k]:
            c.wait()
        for m in range(tiles):
            ms = pl.ds(m * tile, tile)
            lefts[m * len(spans) + k].wait()
            part = jnp.dot(
                lbuf[ms, lo:hi], rbuf[lo:hi, :], preferred_element_type=jnp.float32
            )
            if k:
                part = part + tbuf[ms, :]
            if k < len(spans) - 1:
                tbuf[ms, :] = part
                continue
            if has_acc:
                accs[m].wait()
                part = part + abuf[ms, :].astype(jnp.float32)
            obuf[ms, :] = part.astype(obuf.dtype)
            if has_diag:
                row = lax.broadcasted_iota(jnp.int32, (tile, tile), 0)
                col = lax.broadcasted_iota(jnp.int32, (tile, tile), 1)
                extra = jnp.where(row == col, diag_ref[:, ms], 0.0)
                obuf[ms, ms] = obuf[ms, ms] + extra
            outs[m].start()
    for c in outs:
        c.wait()


def gram(left, slots, pieces, acc=None, diag=None):
    width = left.shape[0]
    n = left.shape[1] // 16
    first = min(slot[0] for slot in slots)
    depth = n * (1 + max(slot[0] for slot in slots) - first)
    cuts = [0, 6 * n, depth] if depth > 6 * n else [0, depth]
    used = sorted({slot[2] for slot in slots})
    slots = [(s, o, used.index(p), r, k) for s, o, p, r, k in slots]
    pieces = [pieces[p] for p in used]
    has_acc, has_diag = acc is not None, diag is not None
    kind = jnp.float32 if has_diag else jnp.bfloat16
    tiles = width // min(256, width)
    anywhere = pl.BlockSpec(memory_space=pl.ANY)
    operands = [left, *pieces]
    in_specs = [anywhere] * len(operands)
    if has_acc:
        operands.append(acc)
        in_specs.append(anywhere)
    if has_diag:
        operands.append(diag)
        in_specs.append(pl.BlockSpec(memory_space=pltpu.VMEM))
    sems = [tiles * (len(cuts) - 1), len(slots), tiles, tiles]
    return pl.pallas_call(
        lambda *refs: gram_kernel(
            slots, first, n, len(pieces), cuts, has_acc, has_diag, *refs
        ),
        out_shape=jax.ShapeDtypeStruct((width, width), kind),
        in_specs=in_specs,
        out_specs=anywhere,
        scratch_shapes=[
            pltpu.VMEM((width, depth), jnp.bfloat16),
            pltpu.VMEM((depth, width), jnp.bfloat16),
            pltpu.VMEM((width if len(cuts) > 2 else 8, width), jnp.float32),
            pltpu.VMEM((width if has_acc else 16, width), jnp.bfloat16),
            pltpu.VMEM((width, width), kind),
            *[pltpu.SemaphoreType.DMA((k,)) for k in sems],
        ],
        compiler_params=pltpu.CompilerParams(vmem_limit_bytes=60 * 2**20),
        cost_estimate=pl.CostEstimate(flops=1, bytes_accessed=1, transcendentals=0),
        name="gram",
    )(*operands)


def per_device(features, labels, posterior, prior_prec):
    n, width = features.shape
    a = n * 5 // 12 // 16 * 16
    b = n - a
    row_index = lax.axis_index("rows")
    feat_index = lax.axis_index("feat")
    core, x, yh = row_index % 2, row_index // 2 % 4, row_index // 8
    z, yl = feat_index % 8, feat_index // 8

    slots, pieces, row = [], [], []

    def put(operand, *parts):
        for slot, offset, source, rows in parts:
            slots.append((slot, offset, len(pieces), source, rows))
        pieces.append(operand)

    for by in (0, -1, 1, -2, 2, -3, 3, 4):
        for yl_ in (yl, 1 - yl):
            d = ((z + by) - row_index) % 8
            x_ = jnp.where(core == 0, d % 4, -d % 4)
            row.append(yl_ * 8 + x_ * 2 + d // 4)
    row = jnp.stack(row).astype(jnp.int32)

    def slot_of(other, dy, dx):
        c_, x_ = core ^ other, (x + dx) % 4
        d = c_ * 4 + jnp.where(core == 0, x_, -x_ % 4)
        by = (d + row_index - z + 3) % 8 - 3
        rank = jnp.where(by < 0, -2 * by - 1, 2 * by)
        rank = jnp.where(by == 4, 7, rank)
        return 2 * rank + (yh ^ dy ^ yl)

    order = [(0, 0), (0, 1), (0, 3), (1, 0), (1, 1), (1, 3), (0, 2), (1, 2)]
    slot = [slot_of(other, dy, dx) for other in range(2) for dy, dx in order]
    slot = jnp.stack(slot).astype(jnp.int32)

    mine = permuted(features, spread)
    partial = jnp.dot(features, posterior, preferred_element_type=jnp.float32)
    across = swap(features, "yh")
    left1, right1 = shift(features, "x", 1), shift(features, "x", -1)
    margins = from_all(partial, "feat").sum(axis=0)
    across, left1, right1, margins, mine = together(
        across, left1, right1, margins, mine
    )

    up1, down1 = shift(mine, "z", 1), shift(mine, "z", -1)
    mine_y = swap(mine, "yl")
    left2, right2 = shift(across, "x", 1), shift(across, "x", -1)
    facts = jnp.stack([margins, labels.astype(jnp.float32)])
    facts = from_all(facts, "rows")
    held = (features, across, left1, right1, prior_prec)
    up1, down1, mine_y, left2, right2, facts, *held = together(
        up1, down1, mine_y, left2, right2, facts, *held
    )
    features, across, left1, right1, prior_prec = held
    chance = jax.nn.sigmoid(facts[:, :1])
    weight = (chance * (1.0 - chance)).astype(jnp.bfloat16).astype(jnp.float32)
    residual = (facts[:, 1:] - chance).astype(jnp.bfloat16)
    diag = jnp.where(row_index == feat_index, prior_prec, 0.0)[None, :]
    put(mine, (0, 0, 0, n))
    put(mine_y, (1, 0, 0, n))

    other_a = mine_y[:a]
    up2 = shift(jnp.concatenate([up1[:a], other_a, up1[a:]]), "z", 1)
    down2 = shift(jnp.concatenate([down1, other_a]), "z", -1)
    swapped1 = swap(jnp.concatenate([up1[a:], down1[a:]]), "yl")
    twice_own, twice_far = shift(left1, "x", 1), shift(right2, "x", -1)
    up2, down2, swapped1, twice_own, twice_far, *small = together(
        up2, down2, swapped1, twice_own, twice_far, weight, residual, diag, slot, row
    )
    weight, residual, diag, slot, row = small
    put(up1, (2, 0, 0, n))
    put(down1, (4, 0, 0, n))
    put(swapped1, (3, a, 0, b), (5, a, b, b))

    up3, down3 = shift(up2, "z", 1), shift(down2, "z", -1)
    swap_u2, swap_d2 = swap(up2[2 * a :], "yl"), swap(down2[a:n], "yl")
    same = [features, right1, left1, across, right2, left2, twice_own, twice_far]
    same = jnp.stack(same)
    other = swap(same, "c")
    left, gradient = prepare(
        slot, row, same, other, weight, residual, prior_prec[None], posterior[None]
    )
    up3, down3, swap_u2, swap_d2, left = together(up3, down3, swap_u2, swap_d2, left)
    put(up2, (6, 0, 0, a), (3, 0, a, a), (6, a, 2 * a, b))
    put(down2, (8, 0, 0, n), (5, 0, n, a))
    put(swap_u2, (7, a, 0, b))
    put(swap_d2, (9, a, 0, b))

    up4 = shift(up3[: 2 * a], "z", 1)
    down4 = shift(down3[a:], "z", -1)
    swap_u3, swap_d3 = swap(up3[2 * a :], "yl"), swap(down3[a:n], "yl")
    put(up3, (10, 0, 0, a), (7, 0, a, a), (10, a, 2 * a, b))
    put(down3, (12, 0, 0, n), (9, 0, n, a))
    put(swap_u3, (11, a, 0, b))
    put(swap_d3, (13, a, 0, b))
    acc = gram(left, [slot for slot in slots if slot[0] < 10], pieces)
    up4, down4, swap_u3, swap_d3, acc = together(up4, down4, swap_u3, swap_d3, acc)

    up5 = shift(up4[a:], "z", 1)
    swapped4 = swap(down4[:b], "yl")
    pieces[-2:] = [swap_u3, swap_d3]
    put(up4, (14, 0, 0, a), (11, 0, a, a))
    put(down4, (14, a, 0, b), (13, 0, b, a))
    acc = gram(left, [slot for slot in slots if 10 <= slot[0] < 14], pieces, acc)
    put(up5, (15, 0, 0, a))
    put(swapped4, (15, a, 0, b))

    last = [slot for slot in slots if slot[0] >= 14]
    hessian = gram(left, last, pieces, acc, diag)
    return (hessian, gradient[0])


def solution(mesh):
    in_specs = (P("rows", "feat"), P("rows"), P("feat"), P("feat"))
    out_specs = (P("feat", "rows"), P("feat"))
    return jax.shard_map(
        per_device, mesh=mesh, in_specs=in_specs, out_specs=out_specs, check_vma=False
    )
```

```python
import jax
import jax.numpy as jnp
from jax import lax
from jax.experimental import pallas as pl
from jax.experimental.pallas import tpu as pltpu
from jax.sharding import PartitionSpec as P

SIZES = dict(yh=2, x=4, c=2, yl=2, z=8)


def place_of(index):
    r, f = divmod(index, 16)
    return dict(yh=r // 8, x=r // 2 % 4, c=r % 2, yl=f // 8, z=f % 8)


def index_of(p):
    return (p["yh"] * 8 + p["x"] * 2 + p["c"]) * 16 + p["yl"] * 8 + p["z"]


def permuted(x, move):
    pairs = [(i, index_of(move(place_of(i)))) for i in range(256)]
    return lax.ppermute(x, ("rows", "feat"), pairs)


def shift(x, axis, by):
    return permuted(x, lambda p: {**p, axis: (p[axis] + by) % SIZES[axis]})


def swap(x, axis):
    return shift(x, axis, 1)


def spread(p):
    flip = p["x"] if p["z"] % 2 == 0 else -p["x"] % 4
    z = (p["z"] + flip + 4 * p["c"]) % 8
    return dict(yh=p["yl"], x=p["z"] // 2, c=p["z"] % 2, yl=p["yh"], z=z)


def from_all(x, axis):
    copies = jnp.broadcast_to(x, (16, *x.shape))
    return lax.all_to_all(copies, axis, split_axis=0, concat_axis=0, tiled=True)


def together(*arrays):
    return lax.optimization_barrier(arrays)


def prepare_kernel(slot_ref, row_ref, *refs):
    same, other = refs[:2]
    weight_ref, residual_ref, prior_ref, point_ref = refs[2:6]
    out_ref, grad_ref, lbuf, obuf, lsem, osem = refs[6:]
    _, n, width = same.shape
    copies = []
    for i in range(16):
        start = pl.multiple_of(slot_ref[i] * n, 16)
        copies.append(
            pltpu.make_async_copy(
                (same if i < 8 else other).at[i % 8],
                lbuf.at[pl.ds(start, n)],
                lsem.at[i],
            )
        )
    for c in copies:
        c.start()
    for c in copies:
        c.wait()
    total = jnp.zeros(grad_ref.shape, jnp.float32)
    outs = []
    for g in range(8):
        block = lbuf[2 * g * n : 2 * (g + 1) * n, :]
        lines = [residual_ref[row_ref[2 * g + i]] for i in range(2)]
        total = total + jnp.dot(
            jnp.concatenate(lines, axis=1), block, preferred_element_type=jnp.float32
        )
        scales = [weight_ref[row_ref[2 * g + i]] for i in range(2)]
        turned = block.T.astype(jnp.float32) * jnp.concatenate(scales, axis=1)
        columns = pl.ds(2 * g * n, 2 * n)
        obuf[:, columns] = turned.astype(jnp.bfloat16)
        outs.append(
            pltpu.make_async_copy(
                obuf.at[:, columns], out_ref.at[:, columns], osem.at[g]
            )
        )
        outs[-1].start()
    grad_ref[...] = total - prior_ref[...] * point_ref[...].astype(jnp.float32)
    for c in outs:
        c.wait()


def prepare(slot, row, same, other, weight, residual, prior, point):
    _, n, width = same.shape
    smem = pl.BlockSpec(memory_space=pltpu.SMEM)
    vmem = pl.BlockSpec(memory_space=pltpu.VMEM)
    anywhere = pl.BlockSpec(memory_space=pl.ANY)
    return pl.pallas_call(
        prepare_kernel,
        in_specs=[smem, smem] + [anywhere] * 2 + [vmem] * 4,
        out_specs=[pl.BlockSpec(memory_space=pltpu.HBM), vmem],
        out_shape=[
            jax.ShapeDtypeStruct((width, 16 * n), jnp.bfloat16),
            jax.ShapeDtypeStruct((1, width), jnp.float32),
        ],
        scratch_shapes=[
            pltpu.VMEM((16 * n, width), jnp.bfloat16),
            pltpu.VMEM((width, 16 * n), jnp.bfloat16),
            pltpu.SemaphoreType.DMA((16,)),
            pltpu.SemaphoreType.DMA((8,)),
        ],
        compiler_params=pltpu.CompilerParams(vmem_limit_bytes=60 * 2**20),
        cost_estimate=pl.CostEstimate(flops=1, bytes_accessed=1, transcendentals=0),
        name="prepare",
    )(slot, row, same, other, weight, residual, prior, point)


def gram_kernel(slots, first, n, count, cuts, has_acc, has_diag, *refs):
    left_ref = refs[0]
    pieces = refs[1 : 1 + count]
    rest = refs[1 + count :]
    if has_acc:
        acc_ref, rest = rest[0], rest[1:]
    if has_diag:
        diag_ref, rest = rest[0], rest[1:]
    out_ref, lbuf, rbuf, tbuf, abuf, obuf, lsem, rsem, asem, osem = rest
    width = obuf.shape[0]
    tile = min(256, width)
    tiles = width // tile
    spans = list(zip(cuts[:-1], cuts[1:]))
    copies = [[] for _ in spans]
    for i, (slot, offset, operand, source, rows) in enumerate(slots):
        at = (slot - first) * n + offset
        span = [k for k, (lo, hi) in enumerate(spans) if lo <= at < hi][0]
        copies[span].append(
            pltpu.make_async_copy(
                pieces[operand].at[pl.ds(source, rows)],
                rbuf.at[pl.ds(at, rows)],
                rsem.at[i],
            )
        )
    lefts, accs, outs = [], [], []
    for m in range(tiles):
        ms = pl.ds(m * tile, tile)
        for k, (lo, hi) in enumerate(spans):
            lefts.append(
                pltpu.make_async_copy(
                    left_ref.at[ms, pl.ds(first * n + lo, hi - lo)],
                    lbuf.at[ms, pl.ds(lo, hi - lo)],
                    lsem.at[m * len(spans) + k],
                )
            )
        if has_acc:
            accs.append(pltpu.make_async_copy(acc_ref.at[ms], abuf.at[ms], asem.at[m]))
        outs.append(pltpu.make_async_copy(obuf.at[ms], out_ref.at[ms], osem.at[m]))
    for k in range(len(spans)):
        lefts[k].start()
        for c in copies[k]:
            c.start()
        for m in range(1, tiles):
            lefts[m * len(spans) + k].start()
    for c in accs:
        c.start()
    for k, (lo, hi) in enumerate(spans):
        for c in copies[k]:
            c.wait()
        for m in range(tiles):
            ms = pl.ds(m * tile, tile)
            lefts[m * len(spans) + k].wait()
            part = jnp.dot(
                lbuf[ms, lo:hi], rbuf[lo:hi, :], preferred_element_type=jnp.float32
            )
            if k:
                part = part + tbuf[ms, :]
            if k < len(spans) - 1:
                tbuf[ms, :] = part
                continue
            if has_acc:
                accs[m].wait()
                part = part + abuf[ms, :].astype(jnp.float32)
            obuf[ms, :] = part.astype(obuf.dtype)
            if has_diag:
                row = lax.broadcasted_iota(jnp.int32, (tile, tile), 0)
                col = lax.broadcasted_iota(jnp.int32, (tile, tile), 1)
                extra = jnp.where(row == col, diag_ref[:, ms], 0.0)
                obuf[ms, ms] = obuf[ms, ms] + extra
            outs[m].start()
    for c in outs:
        c.wait()


def gram(left, slots, pieces, acc=None, diag=None):
    width = left.shape[0]
    n = left.shape[1] // 16
    first = min(slot[0] for slot in slots)
    depth = n * (1 + max(slot[0] for slot in slots) - first)
    cuts = [0, 6 * n, depth] if depth > 6 * n else [0, depth]
    used = sorted({slot[2] for slot in slots})
    slots = [(s, o, used.index(p), r, k) for s, o, p, r, k in slots]
    pieces = [pieces[p] for p in used]
    has_acc, has_diag = acc is not None, diag is not None
    kind = jnp.float32 if has_diag else jnp.bfloat16
    tiles = width // min(256, width)
    anywhere = pl.BlockSpec(memory_space=pl.ANY)
    operands = [left, *pieces]
    in_specs = [anywhere] * len(operands)
    if has_acc:
        operands.append(acc)
        in_specs.append(anywhere)
    if has_diag:
        operands.append(diag)
        in_specs.append(pl.BlockSpec(memory_space=pltpu.VMEM))
    sems = [tiles * (len(cuts) - 1), len(slots), tiles, tiles]
    return pl.pallas_call(
        lambda *refs: gram_kernel(
            slots, first, n, len(pieces), cuts, has_acc, has_diag, *refs
        ),
        out_shape=jax.ShapeDtypeStruct((width, width), kind),
        in_specs=in_specs,
        out_specs=anywhere,
        scratch_shapes=[
            pltpu.VMEM((width, depth), jnp.bfloat16),
            pltpu.VMEM((depth, width), jnp.bfloat16),
            pltpu.VMEM((width if len(cuts) > 2 else 8, width), jnp.float32),
            pltpu.VMEM((width if has_acc else 16, width), jnp.bfloat16),
            pltpu.VMEM((width, width), kind),
            *[pltpu.SemaphoreType.DMA((k,)) for k in sems],
        ],
        compiler_params=pltpu.CompilerParams(vmem_limit_bytes=60 * 2**20),
        cost_estimate=pl.CostEstimate(flops=1, bytes_accessed=1, transcendentals=0),
        name="gram",
    )(*operands)


def per_device(features, labels, posterior, prior_prec):
    n, width = features.shape
    a = n * 5 // 12 // 16 * 16
    b = n - a
    row_index = lax.axis_index("rows")
    feat_index = lax.axis_index("feat")
    core, x, yh = row_index % 2, row_index // 2 % 4, row_index // 8
    z, yl = feat_index % 8, feat_index // 8

    slots, pieces, row = [], [], []

    def put(operand, *parts):
        for slot, offset, source, rows in parts:
            slots.append((slot, offset, len(pieces), source, rows))
        pieces.append(operand)

    for by in (0, -1, 1, -2, 2, -3, 3, 4):
        for yl_ in (yl, 1 - yl):
            d = ((z + by) - row_index) % 8
            x_ = jnp.where(core == 0, d % 4, -d % 4)
            row.append(yl_ * 8 + x_ * 2 + d // 4)
    row = jnp.stack(row).astype(jnp.int32)

    def slot_of(other, dy, dx):
        c_, x_ = core ^ other, (x + dx) % 4
        d = c_ * 4 + jnp.where(core == 0, x_, -x_ % 4)
        by = (d + row_index - z + 3) % 8 - 3
        rank = jnp.where(by < 0, -2 * by - 1, 2 * by)
        rank = jnp.where(by == 4, 7, rank)
        return 2 * rank + (yh ^ dy ^ yl)

    order = [(0, 0), (0, 1), (0, 3), (1, 0), (1, 1), (1, 3), (0, 2), (1, 2)]
    slot = [slot_of(other, dy, dx) for other in range(2) for dy, dx in order]
    slot = jnp.stack(slot).astype(jnp.int32)

    mine = permuted(features, spread)
    partial = jnp.dot(features, posterior, preferred_element_type=jnp.float32)
    across = swap(features, "yh")
    left1, right1 = shift(features, "x", 1), shift(features, "x", -1)
    margins = from_all(partial, "feat").sum(axis=0)
    marks = labels.astype(jnp.float32)
    across, left1, right1, margins, marks, mine = together(
        across, left1, right1, margins, marks, mine
    )

    up1, down1 = shift(mine, "z", 1), shift(mine, "z", -1)
    mine_y = swap(mine, "yl")
    left2, right2 = shift(across, "x", 1), shift(across, "x", -1)
    facts = jnp.stack([margins, marks])
    facts = from_all(facts, "rows")
    held = (features, across, left1, right1, prior_prec)
    up1, down1, mine_y, left2, right2, facts, *held = together(
        up1, down1, mine_y, left2, right2, facts, *held
    )
    features, across, left1, right1, prior_prec = held
    chance = jax.nn.sigmoid(facts[:, :1])
    weight = (chance * (1.0 - chance)).astype(jnp.bfloat16).astype(jnp.float32)
    residual = (facts[:, 1:] - chance).astype(jnp.bfloat16)
    diag = jnp.where(row_index == feat_index, prior_prec, 0.0)[None, :]
    put(mine, (0, 0, 0, n))
    put(mine_y, (1, 0, 0, n))

    other_a = mine_y[:a]
    up2 = shift(jnp.concatenate([up1[:a], other_a, up1[a:]]), "z", 1)
    down2 = shift(jnp.concatenate([down1, other_a]), "z", -1)
    swapped1 = swap(jnp.concatenate([up1[a:], down1[a:]]), "yl")
    twice_own, twice_far = shift(left1, "x", 1), shift(right2, "x", -1)
    up2, down2, swapped1, twice_own, twice_far, *small = together(
        up2, down2, swapped1, twice_own, twice_far, weight, residual, diag, slot, row
    )
    weight, residual, diag, slot, row = small
    put(up1, (2, 0, 0, n))
    put(down1, (4, 0, 0, n))
    put(swapped1, (3, a, 0, b), (5, a, b, b))

    up3, down3 = shift(up2, "z", 1), shift(down2, "z", -1)
    swap_u2, swap_d2 = swap(up2[2 * a :], "yl"), swap(down2[a:n], "yl")
    same = [features, right1, left1, across, right2, left2, twice_own, twice_far]
    same = jnp.stack(same)
    other = swap(same, "c")
    left, gradient = prepare(
        slot, row, same, other, weight, residual, prior_prec[None], posterior[None]
    )
    up3, down3, swap_u2, swap_d2, left = together(up3, down3, swap_u2, swap_d2, left)
    put(up2, (6, 0, 0, a), (3, 0, a, a), (6, a, 2 * a, b))
    put(down2, (8, 0, 0, n), (5, 0, n, a))
    put(swap_u2, (7, a, 0, b))
    put(swap_d2, (9, a, 0, b))

    up4 = shift(up3[: 2 * a], "z", 1)
    down4 = shift(down3[a:], "z", -1)
    swap_u3, swap_d3 = swap(up3[2 * a :], "yl"), swap(down3[a:n], "yl")
    put(up3, (10, 0, 0, a), (7, 0, a, a), (10, a, 2 * a, b))
    put(down3, (12, 0, 0, n), (9, 0, n, a))
    put(swap_u3, (11, a, 0, b))
    put(swap_d3, (13, a, 0, b))
    acc = gram(left, [slot for slot in slots if slot[0] < 10], pieces)
    up4, down4, swap_u3, swap_d3, acc = together(up4, down4, swap_u3, swap_d3, acc)

    up5 = shift(up4[a:], "z", 1)
    swapped4 = swap(down4[:b], "yl")
    pieces[-2:] = [swap_u3, swap_d3]
    put(up4, (14, 0, 0, a), (11, 0, a, a))
    put(down4, (14, a, 0, b), (13, 0, b, a))
    acc = gram(left, [slot for slot in slots if 10 <= slot[0] < 14], pieces, acc)
    put(up5, (15, 0, 0, a))
    put(swapped4, (15, a, 0, b))

    last = [slot for slot in slots if slot[0] >= 14]
    hessian = gram(left, last, pieces, acc, diag)
    return (hessian, gradient[0])


def solution(mesh):
    in_specs = (P("rows", "feat"), P("rows"), P("feat"), P("feat"))
    out_specs = (P("feat", "rows"), P("feat"))
    return jax.shard_map(
        per_device, mesh=mesh, in_specs=in_specs, out_specs=out_specs, check_vma=False
    )
```

```python
import jax
import jax.numpy as jnp
from jax import lax
from jax.experimental import pallas as pl
from jax.experimental.pallas import tpu as pltpu
from jax.sharding import PartitionSpec as P

SIZES = dict(yh=2, x=4, c=2, yl=2, z=8)


def place_of(index):
    r, f = divmod(index, 16)
    return dict(yh=r // 8, x=r // 2 % 4, c=r % 2, yl=f // 8, z=f % 8)


def index_of(p):
    return (p["yh"] * 8 + p["x"] * 2 + p["c"]) * 16 + p["yl"] * 8 + p["z"]


def permuted(x, move):
    pairs = [(i, index_of(move(place_of(i)))) for i in range(256)]
    return lax.ppermute(x, ("rows", "feat"), pairs)


def shift(x, axis, by):
    return permuted(x, lambda p: {**p, axis: (p[axis] + by) % SIZES[axis]})


def swap(x, axis):
    return shift(x, axis, 1)


def spread(p):
    flip = p["x"] if p["z"] % 2 == 0 else -p["x"] % 4
    z = (p["z"] + flip + 4 * p["c"]) % 8
    return dict(yh=p["yl"], x=p["z"] // 2, c=p["z"] % 2, yl=p["yh"], z=z)


def from_all(x, axis):
    copies = jnp.broadcast_to(x, (16, *x.shape))
    return lax.all_to_all(copies, axis, split_axis=0, concat_axis=0, tiled=True)


def together(*arrays):
    return lax.optimization_barrier(arrays)


def prepare_kernel(slot_ref, row_ref, *refs):
    same, other = refs[:2]
    weight_ref, residual_ref, prior_ref, point_ref = refs[2:6]
    out_ref, grad_ref, lbuf, obuf, lsem, osem = refs[6:]
    _, n, width = same.shape
    copies = []
    for i in range(16):
        start = pl.multiple_of(slot_ref[i] * n, 16)
        copies.append(
            pltpu.make_async_copy(
                (same if i < 8 else other).at[i % 8],
                lbuf.at[pl.ds(start, n)],
                lsem.at[i],
            )
        )
    for c in copies:
        c.start()
    for c in copies:
        c.wait()
    total = jnp.zeros(grad_ref.shape, jnp.float32)
    outs = []
    for g in range(8):
        block = lbuf[2 * g * n : 2 * (g + 1) * n, :]
        lines = [residual_ref[row_ref[2 * g + i]] for i in range(2)]
        total = total + jnp.dot(
            jnp.concatenate(lines, axis=1), block, preferred_element_type=jnp.float32
        )
        scales = [weight_ref[row_ref[2 * g + i]] for i in range(2)]
        turned = block.T.astype(jnp.float32) * jnp.concatenate(scales, axis=1)
        columns = pl.ds(2 * g * n, 2 * n)
        obuf[:, columns] = turned.astype(jnp.bfloat16)
        outs.append(
            pltpu.make_async_copy(
                obuf.at[:, columns], out_ref.at[:, columns], osem.at[g]
            )
        )
        outs[-1].start()
    grad_ref[...] = total - prior_ref[...] * point_ref[...].astype(jnp.float32)
    for c in outs:
        c.wait()


def prepare(slot, row, same, other, weight, residual, prior, point):
    _, n, width = same.shape
    smem = pl.BlockSpec(memory_space=pltpu.SMEM)
    vmem = pl.BlockSpec(memory_space=pltpu.VMEM)
    anywhere = pl.BlockSpec(memory_space=pl.ANY)
    return pl.pallas_call(
        prepare_kernel,
        in_specs=[smem, smem] + [anywhere] * 2 + [vmem] * 4,
        out_specs=[pl.BlockSpec(memory_space=pltpu.HBM), vmem],
        out_shape=[
            jax.ShapeDtypeStruct((width, 16 * n), jnp.bfloat16),
            jax.ShapeDtypeStruct((1, width), jnp.float32),
        ],
        scratch_shapes=[
            pltpu.VMEM((16 * n, width), jnp.bfloat16),
            pltpu.VMEM((width, 16 * n), jnp.bfloat16),
            pltpu.SemaphoreType.DMA((16,)),
            pltpu.SemaphoreType.DMA((8,)),
        ],
        compiler_params=pltpu.CompilerParams(vmem_limit_bytes=60 * 2**20),
        cost_estimate=pl.CostEstimate(flops=1, bytes_accessed=1, transcendentals=0),
        name="prepare",
    )(slot, row, same, other, weight, residual, prior, point)


def gram_kernel(slots, first, n, count, cuts, has_acc, has_diag, *refs):
    left_ref = refs[0]
    pieces = refs[1 : 1 + count]
    rest = refs[1 + count :]
    if has_acc:
        acc_ref, rest = rest[0], rest[1:]
    if has_diag:
        diag_ref, rest = rest[0], rest[1:]
    out_ref, lbuf, rbuf, tbuf, abuf, obuf, lsem, rsem, asem, osem = rest
    width = obuf.shape[0]
    tile = min(256, width)
    tiles = width // tile
    spans = list(zip(cuts[:-1], cuts[1:]))
    copies = [[] for _ in spans]
    for i, (slot, offset, operand, source, rows) in enumerate(slots):
        at = (slot - first) * n + offset
        span = [k for k, (lo, hi) in enumerate(spans) if lo <= at < hi][0]
        copies[span].append(
            pltpu.make_async_copy(
                pieces[operand].at[pl.ds(source, rows)],
                rbuf.at[pl.ds(at, rows)],
                rsem.at[i],
            )
        )
    lefts, accs, outs = [], [], []
    for m in range(tiles):
        ms = pl.ds(m * tile, tile)
        for k, (lo, hi) in enumerate(spans):
            lefts.append(
                pltpu.make_async_copy(
                    left_ref.at[ms, pl.ds(first * n + lo, hi - lo)],
                    lbuf.at[ms, pl.ds(lo, hi - lo)],
                    lsem.at[m * len(spans) + k],
                )
            )
        if has_acc:
            accs.append(pltpu.make_async_copy(acc_ref.at[ms], abuf.at[ms], asem.at[m]))
        outs.append(pltpu.make_async_copy(obuf.at[ms], out_ref.at[ms], osem.at[m]))
    for k in range(len(spans)):
        lefts[k].start()
        for c in copies[k]:
            c.start()
        for m in range(1, tiles):
            lefts[m * len(spans) + k].start()
    for c in accs:
        c.start()
    for k, (lo, hi) in enumerate(spans):
        for c in copies[k]:
            c.wait()
        for m in range(tiles):
            ms = pl.ds(m * tile, tile)
            lefts[m * len(spans) + k].wait()
            part = jnp.dot(
                lbuf[ms, lo:hi], rbuf[lo:hi, :], preferred_element_type=jnp.float32
            )
            if k:
                part = part + tbuf[ms, :]
            if k < len(spans) - 1:
                tbuf[ms, :] = part
                continue
            if has_acc:
                accs[m].wait()
                part = part + abuf[ms, :].astype(jnp.float32)
            obuf[ms, :] = part.astype(obuf.dtype)
            if has_diag:
                row = lax.broadcasted_iota(jnp.int32, (tile, tile), 0)
                col = lax.broadcasted_iota(jnp.int32, (tile, tile), 1)
                extra = jnp.where(row == col, diag_ref[:, ms], 0.0)
                obuf[ms, ms] = obuf[ms, ms] + extra
            outs[m].start()
    for c in outs:
        c.wait()


def gram(left, slots, pieces, acc=None, diag=None):
    width = left.shape[0]
    n = left.shape[1] // 16
    first = min(slot[0] for slot in slots)
    depth = n * (1 + max(slot[0] for slot in slots) - first)
    cuts = [0, 6 * n, depth] if depth > 6 * n else [0, depth]
    used = sorted({slot[2] for slot in slots})
    slots = [(s, o, used.index(p), r, k) for s, o, p, r, k in slots]
    pieces = [pieces[p] for p in used]
    has_acc, has_diag = acc is not None, diag is not None
    kind = jnp.float32 if has_diag else jnp.bfloat16
    tiles = width // min(256, width)
    anywhere = pl.BlockSpec(memory_space=pl.ANY)
    operands = [left, *pieces]
    in_specs = [anywhere] * len(operands)
    if has_acc:
        operands.append(acc)
        in_specs.append(anywhere)
    if has_diag:
        operands.append(diag)
        in_specs.append(pl.BlockSpec(memory_space=pltpu.VMEM))
    sems = [tiles * (len(cuts) - 1), len(slots), tiles, tiles]
    return pl.pallas_call(
        lambda *refs: gram_kernel(
            slots, first, n, len(pieces), cuts, has_acc, has_diag, *refs
        ),
        out_shape=jax.ShapeDtypeStruct((width, width), kind),
        in_specs=in_specs,
        out_specs=anywhere,
        scratch_shapes=[
            pltpu.VMEM((width, depth), jnp.bfloat16),
            pltpu.VMEM((depth, width), jnp.bfloat16),
            pltpu.VMEM((width if len(cuts) > 2 else 8, width), jnp.float32),
            pltpu.VMEM((width if has_acc else 16, width), jnp.bfloat16),
            pltpu.VMEM((width, width), kind),
            *[pltpu.SemaphoreType.DMA((k,)) for k in sems],
        ],
        compiler_params=pltpu.CompilerParams(vmem_limit_bytes=60 * 2**20),
        cost_estimate=pl.CostEstimate(flops=1, bytes_accessed=1, transcendentals=0),
        name="gram",
    )(*operands)


def per_device(features, labels, posterior, prior_prec):
    n, width = features.shape
    a = n * 5 // 12 // 16 * 16
    b = n - a
    row_index = lax.axis_index("rows")
    feat_index = lax.axis_index("feat")
    core, x, yh = row_index % 2, row_index // 2 % 4, row_index // 8
    z, yl = feat_index % 8, feat_index // 8

    slots, pieces, row = [], [], []

    def put(operand, *parts):
        for slot, offset, source, rows in parts:
            slots.append((slot, offset, len(pieces), source, rows))
        pieces.append(operand)

    for by in (0, -1, 1, -2, 2, -3, 3, 4):
        for yl_ in (yl, 1 - yl):
            d = ((z + by) - row_index) % 8
            x_ = jnp.where(core == 0, d % 4, -d % 4)
            row.append(yl_ * 8 + x_ * 2 + d // 4)
    row = jnp.stack(row).astype(jnp.int32)

    def slot_of(other, dy, dx):
        c_, x_ = core ^ other, (x + dx) % 4
        d = c_ * 4 + jnp.where(core == 0, x_, -x_ % 4)
        by = (d + row_index - z + 3) % 8 - 3
        rank = jnp.where(by < 0, -2 * by - 1, 2 * by)
        rank = jnp.where(by == 4, 7, rank)
        return 2 * rank + (yh ^ dy ^ yl)

    order = [(0, 0), (0, 1), (0, 3), (1, 0), (1, 1), (1, 3), (0, 2), (1, 2)]
    slot = [slot_of(other, dy, dx) for other in range(2) for dy, dx in order]
    slot = jnp.stack(slot).astype(jnp.int32)

    mine = permuted(features, spread)
    partial = jnp.dot(features, posterior, preferred_element_type=jnp.float32)
    across = swap(features, "yh")
    left1, right1 = shift(features, "x", 1), shift(features, "x", -1)
    margins = from_all(partial, "feat").sum(axis=0)
    marks = labels.astype(jnp.float32)
    across, left1, right1, margins, marks, mine = together(
        across, left1, right1, margins, marks, mine
    )

    up1, down1 = shift(mine, "z", 1), shift(mine, "z", -1)
    mine_y = swap(mine, "yl")
    left2, right2 = shift(across, "x", 1), shift(across, "x", -1)
    facts = jnp.stack([margins, marks])
    facts = from_all(facts, "rows")
    held = (features, across, left1, right1, prior_prec)
    up1, down1, mine_y, left2, right2, facts, *held = together(
        up1, down1, mine_y, left2, right2, facts, *held
    )
    features, across, left1, right1, prior_prec = held
    chance = jax.nn.sigmoid(facts[:, :1])
    weight = (chance * (1.0 - chance)).astype(jnp.bfloat16).astype(jnp.float32)
    residual = (facts[:, 1:] - chance).astype(jnp.bfloat16)
    diag = jnp.where(row_index == feat_index, prior_prec, 0.0)[None, :]
    put(mine, (0, 0, 0, n))
    put(mine_y, (1, 0, 0, n))

    other_a = mine_y[:a]
    up2 = shift(jnp.concatenate([up1[:a], other_a, up1[a:]]), "z", 1)
    down2 = shift(jnp.concatenate([down1, other_a]), "z", -1)
    swapped1 = swap(jnp.concatenate([up1[a:], down1[a:]]), "yl")
    twice_own, twice_far = shift(left1, "x", 1), shift(right2, "x", -1)
    small = (weight, residual, diag, slot, row, prior_prec[None], posterior[None])
    up2, down2, swapped1, twice_own, twice_far, *small = together(
        up2, down2, swapped1, twice_own, twice_far, *small
    )
    weight, residual, diag, slot, row, prior, point = small
    put(up1, (2, 0, 0, n))
    put(down1, (4, 0, 0, n))
    put(swapped1, (3, a, 0, b), (5, a, b, b))

    up3, down3 = shift(up2, "z", 1), shift(down2, "z", -1)
    swap_u2, swap_d2 = swap(up2[2 * a :], "yl"), swap(down2[a:n], "yl")
    same = [features, right1, left1, across, right2, left2, twice_own, twice_far]
    same = jnp.stack(same)
    other = swap(same, "c")
    left, gradient = prepare(
        slot, row, same, other, weight, residual, prior, point
    )
    up3, down3, swap_u2, swap_d2, left = together(up3, down3, swap_u2, swap_d2, left)
    put(up2, (6, 0, 0, a), (3, 0, a, a), (6, a, 2 * a, b))
    put(down2, (8, 0, 0, n), (5, 0, n, a))
    put(swap_u2, (7, a, 0, b))
    put(swap_d2, (9, a, 0, b))

    up4 = shift(up3[: 2 * a], "z", 1)
    down4 = shift(down3[a:], "z", -1)
    swap_u3, swap_d3 = swap(up3[2 * a :], "yl"), swap(down3[a:n], "yl")
    put(up3, (10, 0, 0, a), (7, 0, a, a), (10, a, 2 * a, b))
    put(down3, (12, 0, 0, n), (9, 0, n, a))
    put(swap_u3, (11, a, 0, b))
    put(swap_d3, (13, a, 0, b))
    acc = gram(left, [slot for slot in slots if slot[0] < 10], pieces)
    up4, down4, swap_u3, swap_d3, acc = together(up4, down4, swap_u3, swap_d3, acc)

    up5 = shift(up4[a:], "z", 1)
    swapped4 = swap(down4[:b], "yl")
    pieces[-2:] = [swap_u3, swap_d3]
    put(up4, (14, 0, 0, a), (11, 0, a, a))
    put(down4, (14, a, 0, b), (13, 0, b, a))
    acc = gram(left, [slot for slot in slots if 10 <= slot[0] < 14], pieces, acc)
    put(up5, (15, 0, 0, a))
    put(swapped4, (15, a, 0, b))

    last = [slot for slot in slots if slot[0] >= 14]
    hessian = gram(left, last, pieces, acc, diag)
    return (hessian, gradient[0])


def solution(mesh):
    in_specs = (P("rows", "feat"), P("rows"), P("feat"), P("feat"))
    out_specs = (P("feat", "rows"), P("feat"))
    return jax.shard_map(
        per_device, mesh=mesh, in_specs=in_specs, out_specs=out_specs, check_vma=False
    )
```
